32 devices in a mesh: dp: 4 (over z), graph: 8 (over y, x, core).
Axes of the slice: x: 2, y: 2, z: 4, core: 2. Of those that a mesh axis runs over, the one named last changes fastest.
Arguments:
- features: float32 [4, 128, 3200], P('dp', 'graph'), may hold values from -6 to 6
- cotangent: float32 [4, 128, 1600], P('dp', 'graph'), may hold values from -6 to 6
- rotation: bfloat16 [4, 114, 1536], P('dp', None, 'graph'), may hold values from -2.6875 to 2.6875
- send_left: int32 [4, 64], P('dp', 'graph'), may hold values from 0 to 16, as said below
- send_right: int32 [4, 64], P('dp', 'graph'), may hold values from 0 to 16, as said below
- edge_src: int32 [4, 1536], P('dp', 'graph'), may hold values from 0 to 31, as said below
- edge_tgt: int32 [4, 1536], P('dp', 'graph'), may hold values from 0 to 15, as said below
- w_zero: bfloat16 [640, 832], P('graph'), may hold values from -0.25 to 0.25
- w_one_re: bfloat16 [512, 256], P('graph'), may hold values from -0.1875 to 0.1875
- w_one_im: bfloat16 [512, 256], P('graph'), may hold values from -0.1875 to 0.1875
- w_two_re: bfloat16 [384, 192], P('graph'), may hold values from -0.21875 to 0.21875
- w_two_im: bfloat16 [384, 192], P('graph'), may hold values from -0.21875 to 0.21875
- w_target: bfloat16 [128, 512], P('graph'), may hold values from -0.5 to 0.5
- alpha_vec: bfloat16 [64, 8], P('graph'), may hold values from -0.75 to 0.75
Outputs:
- attended: bfloat16 [4, 128, 1600], P('dp', 'graph')
- grad_features: float32 [4, 128, 3200], P('dp', 'graph')
- grad_zero: float32 [640, 832], P('graph')
- grad_one_re: float32 [512, 256], P('graph')
- grad_one_im: float32 [512, 256], P('graph')
- grad_two_re: float32 [384, 192], P('graph')
- grad_two_im: float32 [384, 192], P('graph')
- grad_target: float32 [128, 512], P('graph')
- grad_alpha: float32 [64, 8], P('graph')
The draws below stay inside these ranges and needn't reach their ends.
Inputs may be any that keep to these rules, and one draw needn't show every extreme that they name: `send_left`: filled slots come first and name distinct atoms; the value 16 marks an empty slot; each list holds 4 or more atoms, and in every cell some slab fills all 8 slots. `send_right`: like send_left. `edge_src`: values below 16 are the slab's own atoms; 16 + k is slot k of slab g-1's send_right, 24 + k slot k of slab g+1's send_left; never an empty slot. `edge_tgt`: every atom of a slab is the target of one edge or more.
All inputs are finite; a program needn't handle non-finite values.
Results may differ from the reference program's by a relative error of at most 0.0085.
Values may be sent and summed in bfloat16 or wider, within the bound.
A program may use at most 128 MiB of HBM per device.

```python
from functools import partial
import jax
import jax.numpy as jnp
from jax import lax

CH = 128
HIDDEN_SIZE = 64
HEADS = 8
ALPHA = 64
ROTS = 114
ATOM_DEV = 16
GHOST = 8
EDGE_DEV = 192
SLABS = 8
ATOMS = 128
EDGES = 1536
CELLS = 4


def ghost_tables(key):
    base = jax.random.fold_in(key, 11)
    keys = jax.random.split(base, 10)
    slab_ids = jnp.arange(SLABS, dtype=jnp.int32)

    def counts_of(first_key, second_key):
        drawn = jax.random.randint(first_key, (CELLS, SLABS), GHOST - GHOST // 2, GHOST + 1, dtype=jnp.int32)
        fullest = jax.random.randint(second_key, (CELLS, 1), 0, SLABS, dtype=jnp.int32)
        return jnp.where(slab_ids[None, :] == fullest, GHOST, drawn)
    count_left = counts_of(keys[0], keys[1])
    count_right = counts_of(keys[2], keys[3])
    base_ids = jnp.broadcast_to(jnp.arange(ATOM_DEV, dtype=jnp.int32), (CELLS * SLABS, ATOM_DEV))
    order_left = jax.random.permutation(keys[4], base_ids, axis=1, independent=True)[:, :GHOST].reshape(CELLS, SLABS, GHOST)
    order_right = jax.random.permutation(keys[5], base_ids, axis=1, independent=True)[:, :GHOST].reshape(CELLS, SLABS, GHOST)
    slots = jnp.arange(GHOST, dtype=jnp.int32)[None, None, :]
    send_left = jnp.where(slots < count_left[:, :, None], order_left, ATOM_DEV)
    send_right = jnp.where(slots < count_right[:, :, None], order_right, ATOM_DEV)
    first_targets = jnp.broadcast_to(jnp.arange(ATOM_DEV, dtype=jnp.int32), (CELLS, SLABS, ATOM_DEV))
    more_targets = jax.random.randint(keys[6], (CELLS, SLABS, EDGE_DEV - ATOM_DEV), 0, ATOM_DEV, dtype=jnp.int32)
    edge_tgt = jnp.concatenate([first_targets, more_targets], axis=2)
    kinds = jax.random.randint(keys[7], (CELLS, SLABS, EDGE_DEV), 0, 4, dtype=jnp.int32)
    local_src = jax.random.randint(keys[8], (CELLS, SLABS, EDGE_DEV), 0, ATOM_DEV, dtype=jnp.int32)
    raw_slot = jax.random.randint(keys[9], (CELLS, SLABS, EDGE_DEV), 0, 1048576, dtype=jnp.int32)
    left_have = jnp.roll(count_right, 1, axis=1)[:, :, None]
    right_have = jnp.roll(count_left, -1, axis=1)[:, :, None]
    ghost_src = jnp.where(kinds == 2, ATOM_DEV + raw_slot % left_have, ATOM_DEV + GHOST + raw_slot % right_have)
    edge_src = jnp.where(kinds < 2, local_src, ghost_src)
    last_src = ATOM_DEV + GHOST + right_have[:, :, 0] - 1
    edge_src = edge_src.at[:, :, EDGE_DEV - 1].set(last_src)
    return (send_left.reshape(CELLS, SLABS * GHOST), send_right.reshape(CELLS, SLABS * GHOST), edge_src.reshape(CELLS, SLABS * EDGE_DEV), edge_tgt.reshape(CELLS, SLABS * EDGE_DEV))


def draw_send_left(key, part):
    return ghost_tables(key)[0]


def draw_send_right(key, part):
    return ghost_tables(key)[1]


def draw_edge_src(key, part):
    return ghost_tables(key)[2]


def draw_edge_tgt(key, part):
    return ghost_tables(key)[3]


def levels(rng, dims, cuts, smallest, top_value):
    loudness, own = 1.0, jax.random.fold_in(rng, 6)
    for dim, blocks in cuts:
        heights = jnp.exp(jax.random.uniform(jax.random.fold_in(own, dim), (blocks,), jnp.float32, smallest / len(cuts), top_value / len(cuts)))
        loudness = loudness * jnp.repeat(heights, dims[dim] // blocks).reshape([-1 if axis == dim else 1 for axis in range(len(dims))])
    return loudness


def gaussian(rng, shape, scale, reach, shards=(), kind=jnp.bfloat16):
    values = scale * jax.random.normal(rng, shape, jnp.float32)
    if shards:
        values = values * levels(rng, shape, shards, -0.22, 0.18)
    return jnp.clip(values, -reach, reach).astype(kind)


def setup_inputs(seed: int = 0) -> dict:
    seeds = jax.random.split(jax.random.key(seed), 15)
    return {
        "features": gaussian(seeds[0], (CELLS, ATOMS, 25 * CH), 1.0, 6.0, ((0, 4), (1, 8)), jnp.float32),
        "cotangent": gaussian(seeds[1], (CELLS, ATOMS, 25 * HIDDEN_SIZE), 1.0, 6.0, ((0, 4), (1, 8)), jnp.float32),
        "rotation": gaussian(seeds[2], (CELLS, ROTS, EDGES), 0.45, 2.6875, ((0, 4), (2, 8))),
        "send_left": draw_send_left(jax.random.fold_in(seeds[14], 71), 0),
        "send_right": draw_send_right(jax.random.fold_in(seeds[14], 71), 0),
        "edge_src": draw_edge_src(jax.random.fold_in(seeds[14], 71), 0),
        "edge_tgt": draw_edge_tgt(jax.random.fold_in(seeds[14], 71), 0),
        "w_zero": gaussian(seeds[7], (5 * CH, 5 * HIDDEN_SIZE + HEADS * ALPHA), (5 * CH) ** -0.5, 0.25, ((0, 8),)),
        "w_one_re": gaussian(seeds[8], (4 * CH, 4 * HIDDEN_SIZE), (8 * CH) ** -0.5, 0.1875, ((0, 8),)),
        "w_one_im": gaussian(seeds[9], (4 * CH, 4 * HIDDEN_SIZE), (8 * CH) ** -0.5, 0.1875, ((0, 8),)),
        "w_two_re": gaussian(seeds[10], (3 * CH, 3 * HIDDEN_SIZE), (6 * CH) ** -0.5, 0.21875, ((0, 8),)),
        "w_two_im": gaussian(seeds[11], (3 * CH, 3 * HIDDEN_SIZE), (6 * CH) ** -0.5, 0.21875, ((0, 8),)),
        "w_target": gaussian(seeds[12], (CH, HEADS * ALPHA), CH ** -0.5, 0.5, ((0, 8),)),
        "alpha_vec": gaussian(seeds[13], (ALPHA, HEADS), ALPHA ** -0.5, 0.75, ((0, 8),)),
    }


def turn_blocks(rotation, edge_count):
    blocks = []
    offset = 0
    for degree in range(1, 5):
        kept_order = min(degree, 2)
        row_count = 2 * kept_order + 1
        column_count = 2 * degree + 1
        piece_block = rotation[offset:offset + row_count * column_count].astype(jnp.float32)
        blocks.append(piece_block.reshape(row_count, column_count, edge_count))
        offset = offset + row_count * column_count
    return blocks

def pick_order(turned, azimuth, degrees, edge_count):
    chosen = jnp.stack([turned[degree][:, min(degree, 2) + azimuth, :] for degree in degrees], axis=1)
    return chosen.reshape(edge_count, -1).astype(jnp.bfloat16)

def attend(extended, w_zero, w_one_re, w_one_im, w_two_re, w_two_im, w_target, alpha_vec, rotation, edge_src, edge_tgt, atom_count):
    edge_count = edge_src.shape[0]
    channels = w_target.shape[0]
    hidden = w_one_re.shape[1] // 4
    head_count = alpha_vec.shape[1]
    alpha_width = alpha_vec.shape[0]
    blocks = turn_blocks(rotation, edge_count)
    coeffs = extended.reshape(extended.shape[0], 25, channels)
    turned = [jnp.take(coeffs[:, 0:1, :], edge_src, axis=0)]
    for degree in range(1, 5):
        source_part = jnp.take(coeffs[:, degree * degree:(degree + 1) * (degree + 1), :], edge_src, axis=0)
        turned.append(jnp.einsum('rne,enc->erc', blocks[degree - 1], source_part, precision=lax.Precision.HIGHEST))
    zero_in = pick_order(turned, 0, range(5), edge_count)
    one_pos = pick_order(turned, 1, range(1, 5), edge_count)
    one_neg = pick_order(turned, -1, range(1, 5), edge_count)
    two_pos = pick_order(turned, 2, range(2, 5), edge_count)
    two_neg = pick_order(turned, -2, range(2, 5), edge_count)
    mixed = jnp.dot(zero_in, w_zero, preferred_element_type=jnp.float32)
    hidden_zero = mixed[:, :5 * hidden].reshape(edge_count, 5, hidden)
    target_in = extended[:atom_count, :channels].astype(jnp.bfloat16)
    per_atom = jnp.dot(target_in, w_target, preferred_element_type=jnp.float32)
    alpha_pre = mixed[:, 5 * hidden:] + jnp.take(per_atom, edge_tgt, axis=0)
    one_up = jnp.dot(one_pos, w_one_re, preferred_element_type=jnp.float32) - jnp.dot(one_neg, w_one_im, preferred_element_type=jnp.float32)
    one_down = jnp.dot(one_neg, w_one_re, preferred_element_type=jnp.float32) + jnp.dot(one_pos, w_one_im, preferred_element_type=jnp.float32)
    two_up = jnp.dot(two_pos, w_two_re, preferred_element_type=jnp.float32) - jnp.dot(two_neg, w_two_im, preferred_element_type=jnp.float32)
    two_down = jnp.dot(two_neg, w_two_re, preferred_element_type=jnp.float32) + jnp.dot(two_pos, w_two_im, preferred_element_type=jnp.float32)
    scalar = hidden_zero[:, 0, :]
    gating = jax.nn.sigmoid(scalar)[:, None, :]
    value_zero = jnp.concatenate([jax.nn.silu(scalar)[:, None, :], hidden_zero[:, 1:, :] * gating], axis=1)
    one_up = one_up.reshape(edge_count, 4, hidden) * gating
    one_down = one_down.reshape(edge_count, 4, hidden) * gating
    two_up = two_up.reshape(edge_count, 3, hidden) * gating
    two_down = two_down.reshape(edge_count, 3, hidden) * gating
    scores = alpha_pre.reshape(edge_count, head_count, alpha_width)
    centre = scores - lax.optimization_barrier(jnp.mean(scores, axis=-1, keepdims=True))
    normed = centre * lax.rsqrt(lax.optimization_barrier(jnp.mean(centre * centre, axis=-1, keepdims=True)) + 1e-05)
    activated = normed * (0.2 + 0.8 * jax.nn.sigmoid(normed))
    logits = jnp.einsum('ehc,ch->eh', activated, alpha_vec.astype(jnp.float32), precision=lax.Precision.HIGHEST)
    raised = jnp.exp(logits)
    member = (edge_tgt[:, None] == jnp.arange(atom_count, dtype=jnp.int32)[None, :]).astype(jnp.float32)
    totals = jnp.dot(member.T, raised, precision=lax.Precision.HIGHEST)
    weights = raised / jnp.take(totals, edge_tgt, axis=0)
    spread = jnp.repeat(weights, hidden // head_count, axis=1)[:, None, :]
    value_zero = value_zero * spread
    one_up = one_up * spread
    one_down = one_down * spread
    two_up = two_up * spread
    two_down = two_down * spread
    pieces = [value_zero[:, 0:1, :]]
    for degree in range(1, 5):
        kept_order = min(degree, 2)
        row_list = []
        for azimuth in range(-kept_order, kept_order + 1):
            if azimuth == 0:
                row_list.append(value_zero[:, degree])
            elif azimuth == 1:
                row_list.append(one_up[:, degree - 1])
            elif azimuth == -1:
                row_list.append(one_down[:, degree - 1])
            elif azimuth == 2:
                row_list.append(two_up[:, degree - 2])
            else:
                row_list.append(two_down[:, degree - 2])
        stacked = jnp.stack(row_list, axis=1)
        pieces.append(jnp.einsum('rne,erc->enc', blocks[degree - 1], stacked, precision=lax.Precision.HIGHEST))
    message = jnp.concatenate(pieces, axis=1).reshape(edge_count, -1).astype(jnp.bfloat16)
    return jnp.dot(member.T.astype(jnp.bfloat16), message, preferred_element_type=jnp.float32)

def take_rows(source_rows, index_list):
    return jnp.take(source_rows, index_list, axis=0)

def add_back(own_rows, right_list, right_grad, left_list, left_grad):
    padded = jnp.concatenate([own_rows, jnp.zeros((1, own_rows.shape[1]), jnp.float32)], axis=0)
    padded = padded.at[right_list].add(right_grad)
    padded = padded.at[left_list].add(left_grad)
    return padded[:own_rows.shape[0]]

def reference(features, cotangent, rotation, send_left, send_right, edge_src, edge_tgt, w_zero, w_one_re, w_one_im, w_two_re, w_two_im, w_target, alpha_vec):
    weight_list = (w_zero, w_one_re, w_one_im, w_two_re, w_two_im, w_target, alpha_vec)
    row_width = features.shape[2]

    def one_cell(carry, cell):
        cell_rows, cell_cot, cell_rot, left_flat, right_flat, src_flat, tgt_flat = cell
        slab_rows = cell_rows.reshape(SLABS, ATOM_DEV, row_width)
        padded = jnp.concatenate([slab_rows, jnp.zeros((SLABS, 1, row_width), jnp.float32)], axis=1)
        left_lists = left_flat.reshape(SLABS, GHOST)
        right_lists = right_flat.reshape(SLABS, GHOST)
        sent_left = jax.vmap(take_rows)(padded, left_lists)
        sent_right = jax.vmap(take_rows)(padded, right_lists)
        from_left = jnp.roll(sent_right, 1, axis=0)
        from_right = jnp.roll(sent_left, -1, axis=0)
        extended = jnp.concatenate([slab_rows, from_left, from_right], axis=1)
        slab_rot = cell_rot.reshape(ROTS, SLABS, EDGE_DEV).transpose(1, 0, 2)
        slab_src = src_flat.reshape(SLABS, EDGE_DEV)
        slab_tgt = tgt_flat.reshape(SLABS, EDGE_DEV)
        slab_cot = cell_cot.reshape(SLABS, ATOM_DEV, -1)

        def one_slab(sums, slab):
            ext_rows, rot_rows, src_rows, tgt_rows, cot_rows = slab
            local_fn = partial(attend, rotation=rot_rows, edge_src=src_rows, edge_tgt=tgt_rows, atom_count=ATOM_DEV)
            summed, pullback = jax.vjp(local_fn, ext_rows, w_zero, w_one_re, w_one_im, w_two_re, w_two_im, w_target, alpha_vec)
            pulled = pullback(cot_rows)
            sums = tuple((running + term.astype(jnp.float32) for running, term in zip(sums, pulled[1:])))
            return (sums, (summed.astype(jnp.bfloat16), pulled[0]))
        carry, outputs = lax.scan(one_slab, carry, (extended, slab_rot, slab_src, slab_tgt, slab_cot))
        attended_slabs, ext_grads = outputs
        own_grads = ext_grads[:, :ATOM_DEV]
        back_left = jnp.roll(ext_grads[:, ATOM_DEV:ATOM_DEV + GHOST], -1, axis=0)
        back_right = jnp.roll(ext_grads[:, ATOM_DEV + GHOST:], 1, axis=0)
        feature_grads = jax.vmap(add_back)(own_grads, right_lists, back_left, left_lists, back_right)
        return (carry, (attended_slabs.reshape(ATOMS, -1), feature_grads.reshape(ATOMS, -1)))
    start = tuple((jnp.zeros(weight.shape, jnp.float32) for weight in weight_list))
    sums, outputs = lax.scan(one_cell, start, (features, cotangent, rotation, send_left, send_right, edge_src, edge_tgt))
    attended, grad_features = outputs
    return (attended, grad_features, sums[0], sums[1], sums[2], sums[3], sums[4], sums[5], sums[6])
```

```python
from functools import partial

import jax
import jax.numpy as jnp
from jax import lax
from jax.experimental import pallas as pl
from jax.experimental.pallas import tpu as pltpu
from jax.sharding import PartitionSpec as P

F32 = jnp.float32
BF16 = jnp.bfloat16
OFFSETS = {1: 0, 2: 9, 3: 34, 4: 69}
DEGREES = (1, 2, 3, 4)
BLOCK_C = 32
BLOCK_H = 16


def slot(degree, azimuth):
    return {0: degree, 1: 4 + degree, -1: 8 + degree, 2: 11 + degree, -2: 14 + degree}[azimuth]


def orders(degree):
    kept = min(degree, 2)
    return range(-kept, kept + 1)


def rot_row(degree, azimuth, column):
    return OFFSETS[degree] + (azimuth + min(degree, 2)) * (2 * degree + 1) + column


def dot(a, b, ca, cb, precision=None):
    return lax.dot_general(
        a, b, (((ca,), (cb,)), ((), ())), preferred_element_type=F32, precision=precision
    )


def compute_kernel(
    ext_ref, cot_ref, rotation_ref, src_ref, tgt_ref,
    wz_ref, w1r_ref, w1i_ref, w2r_ref, w2i_ref, wt_ref, alpha_ref,
    att_ref, own_ref, ghost_ref, gz_ref, g1r_ref, g1i_ref, g2r_ref, g2i_ref, gt_ref, ga_ref,
    rotf, xs, turned, hid, msg, dmsg, scores, dhid, dmixed, dturned, dxs, small, spreads,
):
    edges = rotation_ref.shape[1]
    rows = ext_ref.shape[0]
    atoms = att_ref.shape[0]
    channels = wt_ref.shape[0]
    hidden = w1r_ref.shape[1] // 4
    heads = small.shape[1]
    width = alpha_ref.shape[0] // heads

    rotf[...] = rotation_ref[...].astype(F32)
    src_hot = (
        lax.broadcasted_iota(jnp.int32, (rows, edges), 0) == src_ref[...]
    ).astype(F32).astype(BF16)
    member = (lax.broadcasted_iota(jnp.int32, (atoms, edges), 0) == tgt_ref[...]).astype(F32)
    member_b = member.astype(BF16)

    for k in range(25):
        xs[k] = dot(ext_ref[:, k * channels:(k + 1) * channels], src_hot, 0, 0)
        dmsg[k] = dot(
            cot_ref[:, k * hidden:(k + 1) * hidden].astype(BF16), member_b, 0, 0
        )

    def turn(i, carry):
        part = pl.ds(pl.multiple_of(i * BLOCK_C, BLOCK_C), BLOCK_C)
        turned[0, part, :] = xs[0, part, :].astype(BF16)
        for degree in DEGREES:
            for azimuth in orders(degree):
                total = None
                for n in range(2 * degree + 1):
                    k = rot_row(degree, azimuth, n)
                    term = rotf[k:k + 1, :] * xs[degree * degree + n, part, :]
                    total = term if total is None else total + term
                turned[slot(degree, azimuth), part, :] = total.astype(BF16)
        return carry

    lax.fori_loop(0, channels // BLOCK_C, turn, 0)

    zero_in = turned[0:5].reshape(5 * channels, edges)
    one_pos = turned[5:9].reshape(4 * channels, edges)
    one_neg = turned[9:13].reshape(4 * channels, edges)
    two_pos = turned[13:16].reshape(3 * channels, edges)
    two_neg = turned[16:19].reshape(3 * channels, edges)

    hid[0:5] = dot(wz_ref[:, :5 * hidden], zero_in, 0, 0).reshape(5, hidden, edges)
    per_atom = dot(ext_ref[:atoms, :channels], wt_ref[...], 1, 0)
    high = per_atom.astype(BF16)
    low = (per_atom - high.astype(F32)).astype(BF16)
    scores[...] = (
        dot(wz_ref[:, 5 * hidden:], zero_in, 0, 0)
        + dot(high, member_b, 0, 0)
        + dot(low, member_b, 0, 0)
    )
    hid[5:9] = (dot(w1r_ref[...], one_pos, 0, 0) - dot(w1i_ref[...], one_neg, 0, 0)).reshape(
        4, hidden, edges)
    hid[9:13] = (dot(w1r_ref[...], one_neg, 0, 0) + dot(w1i_ref[...], one_pos, 0, 0)).reshape(
        4, hidden, edges)
    hid[13:16] = (dot(w2r_ref[...], two_pos, 0, 0) - dot(w2i_ref[...], two_neg, 0, 0)).reshape(
        3, hidden, edges)
    hid[16:19] = (dot(w2r_ref[...], two_neg, 0, 0) + dot(w2i_ref[...], two_pos, 0, 0)).reshape(
        3, hidden, edges)

    for h in range(heads):
        part = slice(h * width, (h + 1) * width)
        value = scores[part, :]
        centre = value - jnp.mean(value, axis=0, keepdims=True)
        scale = lax.rsqrt(jnp.mean(centre * centre, axis=0, keepdims=True) + 1e-05)
        normed = centre * scale
        scores[part, :] = normed
        gate = 0.2 + 0.8 * jax.nn.sigmoid(normed)
        small[0, h:h + 1, :] = jnp.sum(
            normed * gate * alpha_ref[part, :], axis=0, keepdims=True
        )
        small[1, h:h + 1, :] = scale

    exact = lax.Precision.HIGHEST
    raised = jnp.exp(small[0])
    totals = dot(dot(raised, member, 1, 1, exact), member, 1, 0, exact)
    weights = raised / totals
    spreads[0] = jnp.broadcast_to(
        weights[:, None, :], (heads, hidden // heads, edges)
    ).reshape(hidden, edges)

    def mix(i, carry):
        part = pl.ds(pl.multiple_of(i * BLOCK_H, BLOCK_H), BLOCK_H)
        spread = spreads[0, part, :]
        scalar = hid[0, part, :]
        gating = jax.nn.sigmoid(scalar)
        silu = scalar * gating
        both = gating * spread
        msg[0, part, :] = (silu * spread).astype(BF16)
        d_first = dmsg[0, part, :]
        inner = jnp.zeros_like(scalar)
        for degree in DEGREES:
            size = 2 * degree + 1
            sums = [None] * size
            for azimuth in orders(degree):
                raw = hid[slot(degree, azimuth), part, :]
                value = raw * both
                back = None
                for n in range(size):
                    k = rot_row(degree, azimuth, n)
                    line = rotf[k:k + 1, :]
                    term = line * value
                    sums[n] = term if sums[n] is None else sums[n] + term
                    other = line * dmsg[degree * degree + n, part, :]
                    back = other if back is None else back + other
                inner = inner + back * raw
                dhid[slot(degree, azimuth), part, :] = (back * both).astype(BF16)
            for n in range(size):
                msg[degree * degree + n, part, :] = sums[n].astype(BF16)
        spreads[1, part, :] = inner * gating + d_first * silu
        d_scalar = d_first * spread * gating * (1.0 + scalar * (1.0 - gating)) + (
            inner * spread * gating * (1.0 - gating)
        )
        dhid[0, part, :] = d_scalar.astype(BF16)
        return carry

    lax.fori_loop(0, hidden // BLOCK_H, mix, 0)

    att_ref[...] = dot(member_b, msg[...].reshape(25 * hidden, edges), 1, 1).astype(BF16)

    d_weights = jnp.sum(
        spreads[1].reshape(heads, hidden // heads, edges), axis=1
    )
    product = weights * d_weights
    d_logits = product - weights * dot(
        dot(product, member, 1, 1, exact), member, 1, 0, exact
    )
    small[0] = d_logits
    for h in range(heads):
        part = slice(h * width, (h + 1) * width)
        normed = scores[part, :]
        sig = jax.nn.sigmoid(normed)
        gate = 0.2 + 0.8 * sig
        d_logit = small[0, h:h + 1, :]
        ga_ref[part, :] = jnp.sum(normed * gate * d_logit, axis=1, keepdims=True)
        d_norm = d_logit * alpha_ref[part, :] * (gate + 0.8 * normed * sig * (1.0 - sig))
        first = jnp.mean(d_norm, axis=0, keepdims=True)
        second = jnp.mean(d_norm * normed, axis=0, keepdims=True)
        d_score = small[1, h:h + 1, :] * (d_norm - first - normed * second)
        dmixed[5 * hidden + h * width:5 * hidden + (h + 1) * width, :] = d_score.astype(BF16)
    dmixed[:5 * hidden, :] = dhid[0:5].reshape(5 * hidden, edges)

    d_per_atom = dot(member_b, dmixed[5 * hidden:, :], 1, 1).astype(BF16)
    gt_ref[...] = dot(ext_ref[:atoms, :channels], d_per_atom, 0, 0).astype(BF16)
    d_target = dot(d_per_atom, wt_ref[...], 1, 1)

    gz_ref[...] = dot(zero_in, dmixed[...], 1, 1).astype(BF16)
    dturned[0:5] = dot(wz_ref[...], dmixed[...], 1, 0).reshape(5, channels, edges)

    def pair(first, count, re_ref, im_ref, gre_ref, gim_ref, pos, neg):
        middle = first + count
        last = middle + count
        up = dhid[first:middle].reshape(count * hidden, edges)
        down = dhid[middle:last].reshape(count * hidden, edges)
        gre_ref[...] = (dot(pos, up, 1, 1) + dot(neg, down, 1, 1)).astype(BF16)
        gim_ref[...] = (dot(pos, down, 1, 1) - dot(neg, up, 1, 1)).astype(BF16)
        dturned[first:middle] = (
            dot(re_ref[...], up, 1, 0) + dot(im_ref[...], down, 1, 0)
        ).reshape(count, channels, edges)
        dturned[middle:last] = (
            dot(re_ref[...], down, 1, 0) - dot(im_ref[...], up, 1, 0)
        ).reshape(count, channels, edges)

    pair(5, 4, w1r_ref, w1i_ref, g1r_ref, g1i_ref, one_pos, one_neg)
    pair(13, 3, w2r_ref, w2i_ref, g2r_ref, g2i_ref, two_pos, two_neg)

    def turn_back(i, carry):
        part = pl.ds(pl.multiple_of(i * BLOCK_C, BLOCK_C), BLOCK_C)
        dxs[0, part, :] = dturned[0, part, :].astype(BF16)
        for degree in DEGREES:
            for n in range(2 * degree + 1):
                total = None
                for azimuth in orders(degree):
                    k = rot_row(degree, azimuth, n)
                    term = rotf[k:k + 1, :] * dturned[slot(degree, azimuth), part, :]
                    total = term if total is None else total + term
                dxs[degree * degree + n, part, :] = total.astype(BF16)
        return carry

    lax.fori_loop(0, channels // BLOCK_C, turn_back, 0)

    ext_grad = dot(src_hot, dxs[...].reshape(25 * channels, edges), 1, 1)
    own_ref[...] = ext_grad[:atoms]
    own_ref[:, :channels] = ext_grad[:atoms, :channels] + d_target
    ghost_ref[...] = ext_grad[atoms:].astype(BF16)


def compute(ext, cot, rotation, src, tgt, wz, w1r, w1i, w2r, w2i, wt, alpha_col, heads):
    edges = rotation.shape[1]
    atoms = cot.shape[0]
    ghosts = ext.shape[0] - atoms
    channels = wt.shape[0]
    hidden = w1r.shape[1] // 4
    shape = jax.ShapeDtypeStruct
    vmem = pl.BlockSpec(memory_space=pltpu.VMEM)
    out_shape = (
        shape((atoms, 25 * hidden), BF16),
        shape((atoms, 25 * channels), F32),
        shape((ghosts, 25 * channels), BF16),
        shape(wz.shape, BF16),
        shape(w1r.shape, BF16),
        shape(w1i.shape, BF16),
        shape(w2r.shape, BF16),
        shape(w2i.shape, BF16),
        shape(wt.shape, BF16),
        shape(alpha_col.shape, F32),
    )
    scratch = [
        pltpu.VMEM(rotation.shape, F32),
        pltpu.VMEM((25, channels, edges), F32),
        pltpu.VMEM((19, channels, edges), BF16),
        pltpu.VMEM((19, hidden, edges), F32),
        pltpu.VMEM((25, hidden, edges), BF16),
        pltpu.VMEM((25, hidden, edges), F32),
        pltpu.VMEM((alpha_col.shape[0], edges), F32),
        pltpu.VMEM((19, hidden, edges), BF16),
        pltpu.VMEM((wz.shape[1], edges), BF16),
        pltpu.VMEM((19, channels, edges), F32),
        pltpu.VMEM((25, channels, edges), BF16),
        pltpu.VMEM((2, heads, edges), F32),
        pltpu.VMEM((2, hidden, edges), F32),
    ]
    return pl.pallas_call(
        compute_kernel,
        out_shape=out_shape,
        in_specs=[vmem] * 12,
        out_specs=[vmem] * 10,
        scratch_shapes=scratch,
        compiler_params=pltpu.CompilerParams(vmem_limit_bytes=56 * 2**20),
        name="slab",
    )(ext, cot, rotation, src, tgt, wz, w1r, w1i, w2r, w2i, wt, alpha_col)


MESH = pl.DeviceIdType.MESH


def greet(n, depth):
    me = lax.axis_index("graph")
    row = lax.axis_index("dp")
    barrier = pltpu.get_barrier_semaphore()
    for d in range(1, n):
        pl.semaphore_signal(
            barrier, inc=1, device_id=(row, lax.rem(me + d, n)), device_id_type=MESH)
    for d in range(1, depth):
        pl.semaphore_signal(
            barrier, inc=1, device_id=(lax.rem(row + d, depth), me), device_id_type=MESH)
    pl.semaphore_wait(barrier, n - 1 + depth - 1)


def gather_kernel(n, count, *refs):
    shards = refs[:count]
    outgoing = refs[count]
    full = refs[count + 1:2 * count + 1]
    ghosts = refs[2 * count + 1]
    send_sem, recv_sem, pass_sem, local_sem, side_send, side_recv = refs[2 * count + 2:]
    me = lax.axis_index("graph")
    row = lax.axis_index("dp")
    half = n // 2
    sibling = me + 1 - 2 * lax.rem(me, 2)
    right, left = lax.rem(me + 1, n), lax.rem(me + n - 1, n)
    greet(n, 1)

    def remote(src, dst, send, recv, target):
        copy = pltpu.make_async_remote_copy(
            src_ref=src, dst_ref=dst, send_sem=send, recv_sem=recv,
            device_id=(row, target), device_id_type=MESH)
        copy.start()
        return copy

    sends = []
    for side, target in ((1, left), (0, right)):
        sends.append(remote(outgoing.at[1 - side], ghosts.at[side], side_send.at[side],
                            side_recv.at[side], target))
    direct = []
    for d in range(1, half):
        target = lax.rem(me + 2 * d, n)
        for w in range(count):
            direct.append(remote(shards[w], full[w].at[me], send_sem.at[d, w],
                                 recv_sem.at[d, w], target))
    locals_ = []
    for w in range(count):
        copy = pltpu.make_async_copy(shards[w], full[w].at[me], local_sem.at[w])
        copy.start()
        locals_.append(copy)
        sends.append(remote(shards[w], full[w].at[me], send_sem.at[0, w],
                            recv_sem.at[0, w], sibling))
    for d in range(1, half):
        source = lax.rem(me + n - 2 * d, n)
        for w in range(count):
            direct[(d - 1) * count + w].wait_recv()
            sends.append(remote(full[w].at[source], full[w].at[source], pass_sem.at[0, d, w],
                                pass_sem.at[1, d, w], sibling))
    for copy in direct:
        copy.wait_send()
    for copy in locals_:
        copy.wait()
    for copy in sends:
        copy.wait()


def gather(n, shards, outgoing):
    count = len(shards)
    vmem = pl.BlockSpec(memory_space=pltpu.VMEM)
    shapes = [jax.ShapeDtypeStruct((n, *s.shape), s.dtype) for s in shards]
    shapes.append(jax.ShapeDtypeStruct(outgoing.shape, outgoing.dtype))
    dma = pltpu.SemaphoreType.DMA
    return pl.pallas_call(
        partial(gather_kernel, n, count),
        out_shape=tuple(shapes),
        in_specs=[vmem] * (count + 1),
        out_specs=[vmem] * (count + 1),
        scratch_shapes=[dma((n // 2, count)), dma((n // 2, count)), dma((2, n // 2, count)),
                        dma((count,)), dma((2,)), dma((2,))],
        compiler_params=pltpu.CompilerParams(collective_id=0, has_side_effects=True),
        name="fetch",
    )(*shards, outgoing)


def reduce_kernel(n, depth, count, *refs):
    terms = refs[:count]
    ghosts = refs[count]
    sums = refs[count + 1:2 * count + 1]
    back = refs[2 * count + 1]
    rest = refs[2 * count + 2:]
    landed = rest[:count]
    partial_sums = rest[count:2 * count]
    arrived = rest[2 * count:3 * count]
    layers = rest[3 * count:4 * count]
    core_send, core_recv, chip_send, chip_recv, deep_send, deep_recv, side_send, side_recv = (
        rest[4 * count:])
    me = lax.axis_index("graph")
    row = lax.axis_index("dp")
    half = n // 2
    parity = lax.rem(me, 2)
    chip = lax.div(me, 2)
    sibling = me + 1 - 2 * parity
    right, left = lax.rem(me + 1, n), lax.rem(me + n - 1, n)
    greet(n, depth)

    def remote(src, dst, send, recv, target):
        copy = pltpu.make_async_remote_copy(
            src_ref=src, dst_ref=dst, send_sem=send, recv_sem=recv,
            device_id=target, device_id_type=MESH)
        copy.start()
        return copy

    order = list(range(1, half)) + [0]
    first = {}
    for d in order:
        spot = lax.rem(chip + d, half)
        for w in range(count):
            first[d, w] = remote(
                terms[w].at[2 * spot + 1 - parity], landed[w].at[d],
                core_send.at[d, w], core_recv.at[d, w], (row, sibling))
    sides = [
        remote(ghosts.at[0], back.at[0], side_send.at[0], side_recv.at[0], (row, left)),
        remote(ghosts.at[1], back.at[1], side_send.at[1], side_recv.at[1], (row, right)),
    ]
    second = {}
    for d in order:
        target = lax.rem(me + 2 * d, n)
        for w in range(count):
            first[d, w].wait_recv()
            partial_sums[w][d] = (
                terms[w][target].astype(F32) + landed[w][d].astype(F32)
            ).astype(BF16)
            if d:
                second[d, w] = remote(
                    partial_sums[w].at[d], arrived[w].at[d],
                    chip_send.at[d, w], chip_recv.at[d, w], (row, target))
    third = {}
    for w in range(count):
        total = partial_sums[w][0].astype(F32)
        for d in range(1, half):
            second[d, w].wait_recv()
            total = total + arrived[w][d].astype(F32)
        layers[w][row] = total.astype(BF16)
        for z in range(1, depth):
            third[z, w] = remote(
                layers[w].at[row], layers[w].at[row],
                deep_send.at[z, w], deep_recv.at[z, w], (lax.rem(row + z, depth), me))
    for w in range(count):
        for z in range(1, depth):
            third[z, w].wait_recv()
        total = layers[w][0].astype(F32)
        for z in range(1, depth):
            total = total + layers[w][z].astype(F32)
        sums[w][...] = total
    for group in (first, second, third):
        for copy in group.values():
            copy.wait_send()
    for copy in sides:
        copy.wait()


def reduce(n, depth, terms, ghosts):
    count = len(terms)
    half = n // 2
    vmem = pl.BlockSpec(memory_space=pltpu.VMEM)
    shapes = [jax.ShapeDtypeStruct(t.shape[1:], F32) for t in terms]
    shapes.append(jax.ShapeDtypeStruct(ghosts.shape, ghosts.dtype))
    dma = pltpu.SemaphoreType.DMA
    groups = [half, half, half, depth]
    scratch = [pltpu.VMEM((g, *t.shape[1:]), BF16) for g in groups for t in terms]
    scratch += [dma((half, count)) for _ in range(4)]
    scratch += [dma((depth, count)) for _ in range(2)]
    scratch += [dma((2,)), dma((2,))]
    return pl.pallas_call(
        partial(reduce_kernel, n, depth, count),
        out_shape=tuple(shapes),
        in_specs=[vmem] * (count + 1),
        out_specs=[vmem] * (count + 1),
        scratch_shapes=scratch,
        compiler_params=pltpu.CompilerParams(collective_id=1, has_side_effects=True),
        name="combine",
    )(*terms, ghosts)


def body(n, depth, features, cotangent, rotation, send_left, send_right, edge_src, edge_tgt,
         *weights):
    own = features[0]
    atoms, width = own.shape
    slots = send_left.shape[1]
    head_width, heads = weights[6].shape[0] * n, weights[6].shape[1]
    own_b = own.astype(BF16)
    lists = jnp.concatenate([send_left[0], send_right[0]])
    ids = jnp.arange(atoms, dtype=jnp.int32)
    pick = (lists[:, None] == ids[None, :]).astype(BF16)
    outgoing = jnp.dot(pick, own_b, preferred_element_type=F32).astype(BF16)
    *full, ghosts = gather(n, weights, outgoing.reshape(2, slots, width))
    full = [f.reshape(-1, f.shape[2]) for f in full]
    extended = jnp.concatenate([own_b, ghosts.reshape(2 * slots, width)], axis=0)
    alpha_col = full[6].astype(F32).T.reshape(-1, 1)
    attended, own_grad, ghost_grad, *terms = compute(
        extended, cotangent[0], rotation[0], edge_src, edge_tgt, *full[:6], alpha_col, heads)
    terms[6] = terms[6].reshape(heads, head_width).T.astype(BF16)
    terms = [t.reshape(n, -1, t.shape[1]) for t in terms]
    *grads, back = reduce(n, depth, terms, ghost_grad.reshape(2, slots, width))
    places = jnp.concatenate([send_right[0], send_left[0]])
    put = (ids[:, None] == places[None, :]).astype(BF16)
    grad_features = own_grad + jnp.dot(
        put, back.reshape(2 * slots, width), preferred_element_type=F32)
    return (attended[None], grad_features[None], *grads)


def solution(mesh):
    cell = P("dp", "graph", None)
    lists = P("dp", "graph")
    shard = P("graph", None)
    in_specs = (cell, cell, P("dp", None, "graph")) + (lists,) * 4 + (shard,) * 7
    out_specs = (cell, cell) + (shard,) * 7
    return jax.shard_map(
        partial(body, mesh.shape["graph"], mesh.shape["dp"]), mesh=mesh,
        in_specs=in_specs, out_specs=out_specs, check_vma=False)
```

```python
from functools import partial

import jax
import jax.numpy as jnp
from jax import lax
from jax.experimental import pallas as pl
from jax.experimental.pallas import tpu as pltpu
from jax.sharding import PartitionSpec as P

F32 = jnp.float32
BF16 = jnp.bfloat16
OFFSETS = {1: 0, 2: 9, 3: 34, 4: 69}
DEGREES = (1, 2, 3, 4)
BLOCK_C = 32
BLOCK_H = 16


def slot(degree, azimuth):
    return {0: degree, 1: 4 + degree, -1: 8 + degree, 2: 11 + degree, -2: 14 + degree}[azimuth]


def orders(degree):
    kept = min(degree, 2)
    return range(-kept, kept + 1)


def rot_row(degree, azimuth, column):
    return OFFSETS[degree] + (azimuth + min(degree, 2)) * (2 * degree + 1) + column


def dot(a, b, ca, cb, precision=None):
    return lax.dot_general(
        a, b, (((ca,), (cb,)), ((), ())), preferred_element_type=F32, precision=precision
    )


def compute_kernel(
    feat_ref, near_ref, cot_ref, rotation_ref, src_ref, tgt_ref,
    wz_ref, w1r_ref, w1i_ref, w2r_ref, w2i_ref, wt_ref, alpha_ref,
    att_ref, own_ref, ghost_ref, gz_ref, g1r_ref, g1i_ref, g2r_ref, g2i_ref, gt_ref, ga_ref,
    ext_ref, alphas, d_alphas, rotf, xs, turned, hid, msg, dmsg, scores, dhid, dmixed, dturned, dxs, small, spreads,
):
    edges = rotation_ref.shape[1]
    rows = ext_ref.shape[0]
    atoms = att_ref.shape[0]
    channels = wt_ref.shape[0]
    hidden = w1r_ref.shape[1] // 4
    heads = small.shape[1]
    width = alphas.shape[0]
    pieces, piece_rows = alpha_ref.shape[:2]

    ext_ref[:atoms, :] = feat_ref[...].astype(BF16)
    ext_ref[atoms:, :] = near_ref[...].astype(F32).reshape(rows - atoms, -1).astype(BF16)
    for j in range(pieces):
        alphas[j * piece_rows:(j + 1) * piece_rows, :] = alpha_ref[j].astype(F32)

    rotf[...] = rotation_ref[...].astype(F32)
    src_hot = (
        lax.broadcasted_iota(jnp.int32, (rows, edges), 0) == src_ref[...]
    ).astype(F32).astype(BF16)
    member = (lax.broadcasted_iota(jnp.int32, (atoms, edges), 0) == tgt_ref[...]).astype(F32)
    member_b = member.astype(BF16)

    for k in range(25):
        xs[k] = dot(ext_ref[:, k * channels:(k + 1) * channels], src_hot, 0, 0)
        dmsg[k] = dot(
            cot_ref[:, k * hidden:(k + 1) * hidden].astype(BF16), member_b, 0, 0
        )

    def turn(i, carry):
        part = pl.ds(pl.multiple_of(i * BLOCK_C, BLOCK_C), BLOCK_C)
        turned[0, part, :] = xs[0, part, :].astype(BF16)
        for degree in DEGREES:
            for azimuth in orders(degree):
                total = None
                for n in range(2 * degree + 1):
                    k = rot_row(degree, azimuth, n)
                    term = rotf[k:k + 1, :] * xs[degree * degree + n, part, :]
                    total = term if total is None else total + term
                turned[slot(degree, azimuth), part, :] = total.astype(BF16)
        return carry

    lax.fori_loop(0, channels // BLOCK_C, turn, 0)

    zero_in = turned[0:5].reshape(5 * channels, edges)
    one_pos = turned[5:9].reshape(4 * channels, edges)
    one_neg = turned[9:13].reshape(4 * channels, edges)
    two_pos = turned[13:16].reshape(3 * channels, edges)
    two_neg = turned[16:19].reshape(3 * channels, edges)

    hid[0:5] = dot(wz_ref[:, :5 * hidden], zero_in, 0, 0).reshape(5, hidden, edges)
    per_atom = dot(ext_ref[:atoms, :channels], wt_ref[...], 1, 0)
    high = per_atom.astype(BF16)
    low = (per_atom - high.astype(F32)).astype(BF16)
    scores[...] = (
        dot(wz_ref[:, 5 * hidden:], zero_in, 0, 0)
        + dot(high, member_b, 0, 0)
        + dot(low, member_b, 0, 0)
    )
    hid[5:9] = (dot(w1r_ref[...], one_pos, 0, 0) - dot(w1i_ref[...], one_neg, 0, 0)).reshape(
        4, hidden, edges)
    hid[9:13] = (dot(w1r_ref[...], one_neg, 0, 0) + dot(w1i_ref[...], one_pos, 0, 0)).reshape(
        4, hidden, edges)
    hid[13:16] = (dot(w2r_ref[...], two_pos, 0, 0) - dot(w2i_ref[...], two_neg, 0, 0)).reshape(
        3, hidden, edges)
    hid[16:19] = (dot(w2r_ref[...], two_neg, 0, 0) + dot(w2i_ref[...], two_pos, 0, 0)).reshape(
        3, hidden, edges)

    for h in range(heads):
        part = slice(h * width, (h + 1) * width)
        value = scores[part, :]
        centre = value - jnp.mean(value, axis=0, keepdims=True)
        scale = lax.rsqrt(jnp.mean(centre * centre, axis=0, keepdims=True) + 1e-05)
        normed = centre * scale
        scores[part, :] = normed
        gate = 0.2 + 0.8 * jax.nn.sigmoid(normed)
        small[0, h:h + 1, :] = jnp.sum(
            normed * gate * alphas[:, h:h + 1], axis=0, keepdims=True
        )
        small[1, h:h + 1, :] = scale

    exact = lax.Precision.HIGHEST
    raised = jnp.exp(small[0])
    totals = dot(dot(raised, member, 1, 1, exact), member, 1, 0, exact)
    weights = raised / totals
    spreads[0] = jnp.broadcast_to(
        weights[:, None, :], (heads, hidden // heads, edges)
    ).reshape(hidden, edges)

    def mix(i, carry):
        part = pl.ds(pl.multiple_of(i * BLOCK_H, BLOCK_H), BLOCK_H)
        spread = spreads[0, part, :]
        scalar = hid[0, part, :]
        gating = jax.nn.sigmoid(scalar)
        silu = scalar * gating
        both = gating * spread
        msg[0, part, :] = (silu * spread).astype(BF16)
        d_first = dmsg[0, part, :]
        inner = jnp.zeros_like(scalar)
        for degree in DEGREES:
            size = 2 * degree + 1
            sums = [None] * size
            for azimuth in orders(degree):
                raw = hid[slot(degree, azimuth), part, :]
                value = raw * both
                back = None
                for n in range(size):
                    k = rot_row(degree, azimuth, n)
                    line = rotf[k:k + 1, :]
                    term = line * value
                    sums[n] = term if sums[n] is None else sums[n] + term
                    other = line * dmsg[degree * degree + n, part, :]
                    back = other if back is None else back + other
                inner = inner + back * raw
                dhid[slot(degree, azimuth), part, :] = (back * both).astype(BF16)
            for n in range(size):
                msg[degree * degree + n, part, :] = sums[n].astype(BF16)
        spreads[1, part, :] = inner * gating + d_first * silu
        d_scalar = d_first * spread * gating * (1.0 + scalar * (1.0 - gating)) + (
            inner * spread * gating * (1.0 - gating)
        )
        dhid[0, part, :] = d_scalar.astype(BF16)
        return carry

    lax.fori_loop(0, hidden // BLOCK_H, mix, 0)

    att_ref[...] = dot(member_b, msg[...].reshape(25 * hidden, edges), 1, 1).astype(BF16)

    d_weights = jnp.sum(
        spreads[1].reshape(heads, hidden // heads, edges), axis=1
    )
    product = weights * d_weights
    d_logits = product - weights * dot(
        dot(product, member, 1, 1, exact), member, 1, 0, exact
    )
    small[0] = d_logits
    for h in range(heads):
        part = slice(h * width, (h + 1) * width)
        normed = scores[part, :]
        sig = jax.nn.sigmoid(normed)
        gate = 0.2 + 0.8 * sig
        d_logit = small[0, h:h + 1, :]
        d_alphas[:, h:h + 1] = jnp.sum(normed * gate * d_logit, axis=1, keepdims=True)
        d_norm = d_logit * alphas[:, h:h + 1] * (gate + 0.8 * normed * sig * (1.0 - sig))
        first = jnp.mean(d_norm, axis=0, keepdims=True)
        second = jnp.mean(d_norm * normed, axis=0, keepdims=True)
        d_score = small[1, h:h + 1, :] * (d_norm - first - normed * second)
        dmixed[5 * hidden + h * width:5 * hidden + (h + 1) * width, :] = d_score.astype(BF16)
        scores[part, :] = d_score
    for j in range(pieces):
        ga_ref[j] = d_alphas[j * piece_rows:(j + 1) * piece_rows, :].astype(BF16)
    dmixed[:5 * hidden, :] = dhid[0:5].reshape(5 * hidden, edges)

    d_per_atom = dot(member, scores[...], 1, 1, exact).astype(BF16)
    gt_ref[...] = dot(ext_ref[:atoms, :channels], d_per_atom, 0, 0).astype(BF16)
    d_target = dot(d_per_atom, wt_ref[...], 1, 1)

    gz_ref[...] = dot(zero_in, dmixed[...], 1, 1).astype(BF16)
    dturned[0:5] = dot(wz_ref[...], dmixed[...], 1, 0).reshape(5, channels, edges)

    def pair(first, count, re_ref, im_ref, gre_ref, gim_ref, pos, neg):
        middle = first + count
        last = middle + count
        up = dhid[first:middle].reshape(count * hidden, edges)
        down = dhid[middle:last].reshape(count * hidden, edges)
        gre_ref[...] = (dot(pos, up, 1, 1) + dot(neg, down, 1, 1)).astype(BF16)
        gim_ref[...] = (dot(pos, down, 1, 1) - dot(neg, up, 1, 1)).astype(BF16)
        dturned[first:middle] = (
            dot(re_ref[...], up, 1, 0) + dot(im_ref[...], down, 1, 0)
        ).reshape(count, channels, edges)
        dturned[middle:last] = (
            dot(re_ref[...], down, 1, 0) - dot(im_ref[...], up, 1, 0)
        ).reshape(count, channels, edges)

    pair(5, 4, w1r_ref, w1i_ref, g1r_ref, g1i_ref, one_pos, one_neg)
    pair(13, 3, w2r_ref, w2i_ref, g2r_ref, g2i_ref, two_pos, two_neg)

    def turn_back(i, carry):
        part = pl.ds(pl.multiple_of(i * BLOCK_C, BLOCK_C), BLOCK_C)
        dxs[0, part, :] = dturned[0, part, :].astype(BF16)
        for degree in DEGREES:
            for n in range(2 * degree + 1):
                total = None
                for azimuth in orders(degree):
                    k = rot_row(degree, azimuth, n)
                    term = rotf[k:k + 1, :] * dturned[slot(degree, azimuth), part, :]
                    total = term if total is None else total + term
                dxs[degree * degree + n, part, :] = total.astype(BF16)
        return carry

    lax.fori_loop(0, channels // BLOCK_C, turn_back, 0)

    ext_grad = dot(src_hot, dxs[...].reshape(25 * channels, edges), 1, 1)
    own_ref[...] = ext_grad[:atoms]
    own_ref[:, :channels] = ext_grad[:atoms, :channels] + d_target
    slots = ghost_ref.shape[1]
    for side in range(2):
        begin = atoms + side * slots
        ghost_ref[side] = ext_grad[begin:begin + slots].astype(BF16)


def compute(features, near, cot, rotation, src, tgt, wz, w1r, w1i, w2r, w2i, wt, alpha):
    edges = rotation.shape[1]
    atoms = cot.shape[0]
    pieces, piece_rows, heads = alpha.shape
    head_width = pieces * piece_rows
    channels = wt.shape[0]
    hidden = w1r.shape[1] // 4
    shape = jax.ShapeDtypeStruct
    vmem = pl.BlockSpec(memory_space=pltpu.VMEM)
    out_shape = (
        shape((atoms, 25 * hidden), BF16),
        shape((atoms, 25 * channels), F32),
        shape(near.shape, BF16),
        shape(wz.shape, BF16),
        shape(w1r.shape, BF16),
        shape(w1i.shape, BF16),
        shape(w2r.shape, BF16),
        shape(w2i.shape, BF16),
        shape(wt.shape, BF16),
        shape(alpha.shape, BF16),
    )
    scratch = [
        pltpu.VMEM((atoms + 2 * near.shape[1], 25 * channels), BF16),
        pltpu.VMEM((head_width, heads), F32),
        pltpu.VMEM((head_width, heads), F32),
        pltpu.VMEM(rotation.shape, F32),
        pltpu.VMEM((25, channels, edges), F32),
        pltpu.VMEM((19, channels, edges), BF16),
        pltpu.VMEM((19, hidden, edges), F32),
        pltpu.VMEM((25, hidden, edges), BF16),
        pltpu.VMEM((25, hidden, edges), F32),
        pltpu.VMEM((head_width * heads, edges), F32),
        pltpu.VMEM((19, hidden, edges), BF16),
        pltpu.VMEM((wz.shape[1], edges), BF16),
        pltpu.VMEM((19, channels, edges), F32),
        pltpu.VMEM((25, channels, edges), BF16),
        pltpu.VMEM((2, heads, edges), F32),
        pltpu.VMEM((2, hidden, edges), F32),
    ]
    return pl.pallas_call(
        compute_kernel,
        out_shape=out_shape,
        in_specs=[vmem] * 13,
        out_specs=[vmem] * 10,
        scratch_shapes=scratch,
        compiler_params=pltpu.CompilerParams(vmem_limit_bytes=56 * 2**20),
        name="slab",
    )(features, near, cot, rotation, src, tgt, wz, w1r, w1i, w2r, w2i, wt, alpha)


MESH = pl.DeviceIdType.MESH


def greet(n, depth):
    me = lax.axis_index("graph")
    row = lax.axis_index("dp")
    barrier = pltpu.get_barrier_semaphore()
    for d in range(1, n):
        pl.semaphore_signal(
            barrier, inc=1, device_id=(row, lax.rem(me + d, n)), device_id_type=MESH)
    for d in range(1, depth):
        pl.semaphore_signal(
            barrier, inc=1, device_id=(lax.rem(row + d, depth), me), device_id_type=MESH)
    pl.semaphore_wait(barrier, n - 1 + depth - 1)


def gather_kernel(n, count, *refs):
    shards = refs[:count]
    feat_ref, left_ref, right_ref = refs[count:count + 3]
    full = refs[count + 3:2 * count + 3]
    ghosts = refs[2 * count + 3]
    outgoing, send_sem, recv_sem, pass_sem, local_sem, side_send, side_recv = refs[2 * count + 4:]
    me = lax.axis_index("graph")
    row = lax.axis_index("dp")
    half = n // 2
    sibling = me + 1 - 2 * lax.rem(me, 2)
    right, left = lax.rem(me + 1, n), lax.rem(me + n - 1, n)
    own = feat_ref[...].astype(BF16)
    for side, list_ref in ((0, left_ref), (1, right_ref)):
        ids = lax.broadcasted_iota(jnp.int32, (own.shape[0], list_ref.shape[1]), 0)
        pick = (ids == list_ref[...]).astype(F32).astype(BF16)
        outgoing[side] = dot(pick, own, 0, 0).astype(BF16)
    greet(n, 1)

    def remote(src, dst, send, recv, target):
        copy = pltpu.make_async_remote_copy(
            src_ref=src, dst_ref=dst, send_sem=send, recv_sem=recv,
            device_id=(row, target), device_id_type=MESH)
        copy.start()
        return copy

    sends = []
    direct = []
    for d in range(1, half):
        target = lax.rem(me + 2 * d, n)
        for w in range(count):
            direct.append(remote(shards[w], full[w].at[me], send_sem.at[d, w],
                                 recv_sem.at[d, w], target))
    locals_ = []
    for w in range(count):
        copy = pltpu.make_async_copy(shards[w], full[w].at[me], local_sem.at[w])
        copy.start()
        locals_.append(copy)
        sends.append(remote(shards[w], full[w].at[me], send_sem.at[0, w],
                            recv_sem.at[0, w], sibling))
    for side, target in ((1, left), (0, right)):
        sends.append(remote(outgoing.at[1 - side], ghosts.at[side], side_send.at[side],
                            side_recv.at[side], target))
    for d in range(1, half):
        source = lax.rem(me + n - 2 * d, n)
        for w in range(count):
            direct[(d - 1) * count + w].wait_recv()
            sends.append(remote(full[w].at[source], full[w].at[source], pass_sem.at[0, d, w],
                                pass_sem.at[1, d, w], sibling))
    for copy in direct:
        copy.wait_send()
    for copy in locals_:
        copy.wait()
    for copy in sends:
        copy.wait()


def gather(n, shards, features, send_left, send_right):
    count = len(shards)
    vmem = pl.BlockSpec(memory_space=pltpu.VMEM)
    shapes = [jax.ShapeDtypeStruct((n, *s.shape), s.dtype) for s in shards]
    ghosts = (2, send_left.shape[1], features.shape[1])
    shapes.append(jax.ShapeDtypeStruct(ghosts, BF16))
    dma = pltpu.SemaphoreType.DMA
    return pl.pallas_call(
        partial(gather_kernel, n, count),
        out_shape=tuple(shapes),
        in_specs=[vmem] * (count + 3),
        out_specs=[vmem] * (count + 1),
        scratch_shapes=[pltpu.VMEM(ghosts, BF16),
                        dma((n // 2, count)), dma((n // 2, count)), dma((2, n // 2, count)),
                        dma((count,)), dma((2,)), dma((2,))],
        compiler_params=pltpu.CompilerParams(collective_id=0, has_side_effects=True),
        name="fetch",
    )(*shards, features, send_left, send_right)


def reduce_kernel(n, depth, count, *refs):
    terms = refs[:count]
    ghosts = refs[count]
    final = refs[count + 1:2 * count + 1]
    back = refs[2 * count + 1]
    rest = refs[2 * count + 2:]
    landed = rest[:count]
    partial_sums = rest[count:2 * count]
    arrived = rest[2 * count:3 * count]
    layers = rest[3 * count:4 * count]
    incoming = rest[4 * count:5 * count]
    (core_send, core_recv, chip_send, chip_recv, deep_send, deep_recv, last_send, last_recv,
     side_send, side_recv) = rest[5 * count:]
    me = lax.axis_index("graph")
    row = lax.axis_index("dp")
    half = n // 2
    parity = lax.rem(me, 2)
    chip = lax.div(me, 2)
    sibling = me + 1 - 2 * parity
    right, left = lax.rem(me + 1, n), lax.rem(me + n - 1, n)
    greet(n, depth)

    def remote(src, dst, send, recv, target):
        copy = pltpu.make_async_remote_copy(
            src_ref=src, dst_ref=dst, send_sem=send, recv_sem=recv,
            device_id=target, device_id_type=MESH)
        copy.start()
        return copy

    order = list(range(1, half)) + [0]
    first, second, third, fourth = {}, {}, {}, {}
    for w in range(count):
        for d in order:
            spot = lax.rem(chip + d, half)
            first[d, w] = remote(
                terms[w].at[2 * spot + 1 - parity], landed[w].at[d],
                core_send.at[d, w], core_recv.at[d, w], (row, sibling))
    for w in range(count):
        for d in order:
            target = lax.rem(me + 2 * d, n)
            first[d, w].wait_recv()
            partial_sums[w][d] = (
                terms[w][target].astype(F32) + landed[w][d].astype(F32)
            ).astype(BF16)
            if d:
                second[d, w] = remote(
                    partial_sums[w].at[d], arrived[w].at[d],
                    chip_send.at[d, w], chip_recv.at[d, w], (row, target))
    sides = [
        remote(ghosts.at[0], back.at[0], side_send.at[0], side_recv.at[0], (row, left)),
        remote(ghosts.at[1], back.at[1], side_send.at[1], side_recv.at[1], (row, right)),
    ]
    split = [final[w].shape[1] != terms[w].shape[1]
             for w in range(count)]
    for w in range(count):
        total = partial_sums[w][0].astype(F32)
        for d in range(1, half):
            second[d, w].wait_recv()
            total = total + arrived[w][d].astype(F32)
        if split[w]:
            size = total.shape[0] // depth
            for k in range(depth):
                layers[w][k] = total[k * size:(k + 1) * size].astype(BF16)
            for z in range(1, depth):
                target = lax.rem(row + z, depth)
                third[z, w] = remote(
                    layers[w].at[target], incoming[w].at[z],
                    deep_send.at[z, w], deep_recv.at[z, w], (target, me))
        else:
            final[w][row] = total.astype(BF16)
    for w in range(count):
        if split[w]:
            total = layers[w][row].astype(F32)
            for z in range(1, depth):
                third[z, w].wait_recv()
                total = total + incoming[w][z].astype(F32)
            final[w][row] = total.astype(BF16)
        for z in range(1, depth):
            fourth[z, w] = remote(
                final[w].at[row], final[w].at[row],
                last_send.at[z, w], last_recv.at[z, w], (lax.rem(row + z, depth), me))
    for group in (first, second, third):
        for copy in group.values():
            copy.wait_send()
    for copy in sides:
        copy.wait()
    for copy in fourth.values():
        copy.wait()


def reduce(n, depth, terms, ghosts):
    count = len(terms)
    half = n // 2
    vmem = pl.BlockSpec(memory_space=pltpu.VMEM)

    def layered(t):
        rows = t.shape[1] if t.shape[1] % depth else t.shape[1] // depth
        return (depth, rows, t.shape[2])

    shapes = [jax.ShapeDtypeStruct(layered(t), BF16) for t in terms]
    shapes.append(jax.ShapeDtypeStruct(ghosts.shape, ghosts.dtype))
    dma = pltpu.SemaphoreType.DMA
    scratch = [pltpu.VMEM((half, *t.shape[1:]), BF16) for _ in range(3) for t in terms]
    scratch += [pltpu.VMEM(layered(t), BF16) for _ in range(2) for t in terms]
    scratch += [dma((half, count)) for _ in range(4)]
    scratch += [dma((depth, count)) for _ in range(4)]
    scratch += [dma((2,)), dma((2,))]
    return pl.pallas_call(
        partial(reduce_kernel, n, depth, count),
        out_shape=tuple(shapes),
        in_specs=[vmem] * (count + 1),
        out_specs=[vmem] * (count + 1),
        scratch_shapes=scratch,
        compiler_params=pltpu.CompilerParams(collective_id=1, has_side_effects=True),
        name="combine",
    )(*terms, ghosts)


def finish_kernel(count, *refs):
    own_ref, back_ref, left_ref, right_ref = refs[:4]
    final = refs[4:4 + count]
    out_ref = refs[4 + count]
    grads = refs[5 + count:]
    total = own_ref[...]
    for side, list_ref in ((0, right_ref), (1, left_ref)):
        ids = lax.broadcasted_iota(jnp.int32, (total.shape[0], list_ref.shape[1]), 0)
        put = (ids == list_ref[...]).astype(F32).astype(BF16)
        total = total + dot(put, back_ref[side], 1, 0)
    out_ref[...] = total
    for source, grad in zip(final, grads):
        depth, size = source.shape[:2]
        if size == grad.shape[0]:
            value = source[0].astype(F32)
            for k in range(1, depth):
                value = value + source[k].astype(F32)
            grad[...] = value
        else:
            for k in range(depth):
                grad[k * size:(k + 1) * size, :] = source[k].astype(F32)


def finish(own, back, send_left, send_right, final, weights):
    count = len(final)
    vmem = pl.BlockSpec(memory_space=pltpu.VMEM)
    shapes = [jax.ShapeDtypeStruct(own.shape, F32)]
    shapes += [jax.ShapeDtypeStruct(w.shape, F32) for w in weights]
    return pl.pallas_call(
        partial(finish_kernel, count),
        out_shape=tuple(shapes),
        in_specs=[vmem] * (count + 4),
        out_specs=[vmem] * (count + 1),
        name="finish",
    )(own, back, send_left, send_right, *final)


def body(n, depth, features, cotangent, rotation, send_left, send_right, edge_src, edge_tgt,
         *weights):
    *full, near = gather(n, weights, features[0], send_left, send_right)
    matrices = [f.reshape(-1, f.shape[2]) for f in full[:6]]
    attended, own_grad, ghost_grad, *terms = compute(
        features[0], near, cotangent[0], rotation[0], edge_src, edge_tgt, *matrices, full[6])
    terms = [t.reshape(n, -1, t.shape[-1]) for t in terms]
    *final, back = reduce(n, depth, terms, ghost_grad)
    grad_features, *grads = finish(own_grad, back, send_left, send_right, final, weights)
    return (attended[None], grad_features[None], *grads)


def solution(mesh):
    cell = P("dp", "graph", None)
    lists = P("dp", "graph")
    shard = P("graph", None)
    in_specs = (cell, cell, P("dp", None, "graph")) + (lists,) * 4 + (shard,) * 7
    out_specs = (cell, cell) + (shard,) * 7
    return jax.shard_map(
        partial(body, mesh.shape["graph"], mesh.shape["dp"]), mesh=mesh,
        in_specs=in_specs, out_specs=out_specs, check_vma=False)
```

```python
from functools import partial

import jax
import jax.numpy as jnp
from jax import lax
from jax.experimental import pallas as pl
from jax.experimental.pallas import tpu as pltpu
from jax.sharding import PartitionSpec as P

F32 = jnp.float32
BF16 = jnp.bfloat16
OFFSETS = {1: 0, 2: 9, 3: 34, 4: 69}
DEGREES = (1, 2, 3, 4)
BLOCK_C = 32
BLOCK_H = 16


def slot(degree, azimuth):
    return {0: degree, 1: 4 + degree, -1: 8 + degree, 2: 11 + degree, -2: 14 + degree}[azimuth]


def orders(degree):
    kept = min(degree, 2)
    return range(-kept, kept + 1)


def rot_row(degree, azimuth, column):
    return OFFSETS[degree] + (azimuth + min(degree, 2)) * (2 * degree + 1) + column


def dot(a, b, ca, cb, precision=None):
    return lax.dot_general(
        a, b, (((ca,), (cb,)), ((), ())), preferred_element_type=F32, precision=precision
    )


def compute_kernel(
    feat_ref, near_ref, cot_ref, rotation_ref, src_ref, tgt_ref,
    wz_ref, w1r_ref, w1i_ref, w2r_ref, w2i_ref, wt_ref, alpha_ref,
    att_ref, own_ref, ghost_ref, gz_ref, g1r_ref, g1i_ref, g2r_ref, g2i_ref, gt_ref, ga_ref,
    ext_ref, alphas, d_alphas, rotf, xs, turned, hid, msg, dmsg, scores, dhid, dmixed, dturned, dxs, small, spreads,
):
    edges, entries = rotation_ref.shape
    rows = ext_ref.shape[0]
    atoms = att_ref.shape[0]
    channels = wt_ref.shape[0]
    hidden = w1r_ref.shape[1] // 4
    heads = small.shape[1]
    width = alphas.shape[0]
    pieces, piece_rows = alpha_ref.shape[:2]

    ext_ref[:atoms, :] = feat_ref[...].astype(BF16)
    ext_ref[atoms:, :] = near_ref[...].astype(F32).reshape(rows - atoms, -1).astype(BF16)
    for j in range(pieces):
        alphas[j * piece_rows:(j + 1) * piece_rows, :] = alpha_ref[j].astype(F32)

    diagonal = (
        lax.broadcasted_iota(jnp.int32, (entries, entries), 0)
        == lax.broadcasted_iota(jnp.int32, (entries, entries), 1)
    ).astype(F32).astype(BF16)
    rotf[...] = dot(diagonal, rotation_ref[...], 1, 1)
    src_hot = (
        lax.broadcasted_iota(jnp.int32, (rows, edges), 0) == src_ref[...]
    ).astype(F32).astype(BF16)
    member = (lax.broadcasted_iota(jnp.int32, (atoms, edges), 0) == tgt_ref[...]).astype(F32)
    member_b = member.astype(BF16)

    for k in range(25):
        xs[k] = dot(ext_ref[:, k * channels:(k + 1) * channels], src_hot, 0, 0)
        dmsg[k] = dot(
            cot_ref[:, k * hidden:(k + 1) * hidden].astype(BF16), member_b, 0, 0
        )

    def turn(i, carry):
        part = pl.ds(pl.multiple_of(i * BLOCK_C, BLOCK_C), BLOCK_C)
        turned[0, part, :] = xs[0, part, :].astype(BF16)
        for degree in DEGREES:
            for azimuth in orders(degree):
                total = None
                for n in range(2 * degree + 1):
                    k = rot_row(degree, azimuth, n)
                    term = rotf[k:k + 1, :] * xs[degree * degree + n, part, :]
                    total = term if total is None else total + term
                turned[slot(degree, azimuth), part, :] = total.astype(BF16)
        return carry

    lax.fori_loop(0, channels // BLOCK_C, turn, 0)

    zero_in = turned[0:5].reshape(5 * channels, edges)
    one_pos = turned[5:9].reshape(4 * channels, edges)
    one_neg = turned[9:13].reshape(4 * channels, edges)
    two_pos = turned[13:16].reshape(3 * channels, edges)
    two_neg = turned[16:19].reshape(3 * channels, edges)

    hid[0:5] = dot(wz_ref[:, :5 * hidden], zero_in, 0, 0).reshape(5, hidden, edges)
    per_atom = dot(ext_ref[:atoms, :channels], wt_ref[...], 1, 0)
    high = per_atom.astype(BF16)
    low = (per_atom - high.astype(F32)).astype(BF16)
    scores[...] = (
        dot(wz_ref[:, 5 * hidden:], zero_in, 0, 0)
        + dot(high, member_b, 0, 0)
        + dot(low, member_b, 0, 0)
    )
    hid[5:9] = (dot(w1r_ref[...], one_pos, 0, 0) - dot(w1i_ref[...], one_neg, 0, 0)).reshape(
        4, hidden, edges)
    hid[9:13] = (dot(w1r_ref[...], one_neg, 0, 0) + dot(w1i_ref[...], one_pos, 0, 0)).reshape(
        4, hidden, edges)
    hid[13:16] = (dot(w2r_ref[...], two_pos, 0, 0) - dot(w2i_ref[...], two_neg, 0, 0)).reshape(
        3, hidden, edges)
    hid[16:19] = (dot(w2r_ref[...], two_neg, 0, 0) + dot(w2i_ref[...], two_pos, 0, 0)).reshape(
        3, hidden, edges)

    for h in range(heads):
        part = slice(h * width, (h + 1) * width)
        value = scores[part, :]
        centre = value - jnp.mean(value, axis=0, keepdims=True)
        scale = lax.rsqrt(jnp.mean(centre * centre, axis=0, keepdims=True) + 1e-05)
        normed = centre * scale
        scores[part, :] = normed
        gate = 0.2 + 0.8 * jax.nn.sigmoid(normed)
        small[0, h:h + 1, :] = jnp.sum(
            normed * gate * alphas[:, h:h + 1], axis=0, keepdims=True
        )
        small[1, h:h + 1, :] = scale

    exact = lax.Precision.HIGHEST
    raised = jnp.exp(small[0])
    totals = dot(dot(raised, member, 1, 1, exact), member, 1, 0, exact)
    weights = raised / totals
    spreads[0] = jnp.broadcast_to(
        weights[:, None, :], (heads, hidden // heads, edges)
    ).reshape(hidden, edges)

    def mix(i, carry):
        part = pl.ds(pl.multiple_of(i * BLOCK_H, BLOCK_H), BLOCK_H)
        spread = spreads[0, part, :]
        scalar = hid[0, part, :]
        gating = jax.nn.sigmoid(scalar)
        silu = scalar * gating
        both = gating * spread
        msg[0, part, :] = (silu * spread).astype(BF16)
        d_first = dmsg[0, part, :]
        inner = jnp.zeros_like(scalar)
        for degree in DEGREES:
            size = 2 * degree + 1
            sums = [None] * size
            for azimuth in orders(degree):
                raw = hid[slot(degree, azimuth), part, :]
                value = raw * both
                back = None
                for n in range(size):
                    k = rot_row(degree, azimuth, n)
                    line = rotf[k:k + 1, :]
                    term = line * value
                    sums[n] = term if sums[n] is None else sums[n] + term
                    other = line * dmsg[degree * degree + n, part, :]
                    back = other if back is None else back + other
                inner = inner + back * raw
                dhid[slot(degree, azimuth), part, :] = (back * both).astype(BF16)
            for n in range(size):
                msg[degree * degree + n, part, :] = sums[n].astype(BF16)
        spreads[1, part, :] = inner * gating + d_first * silu
        d_scalar = d_first * spread * gating * (1.0 + scalar * (1.0 - gating)) + (
            inner * spread * gating * (1.0 - gating)
        )
        dhid[0, part, :] = d_scalar.astype(BF16)
        return carry

    lax.fori_loop(0, hidden // BLOCK_H, mix, 0)

    att_ref[...] = dot(member_b, msg[...].reshape(25 * hidden, edges), 1, 1).astype(BF16)

    d_weights = jnp.sum(
        spreads[1].reshape(heads, hidden // heads, edges), axis=1
    )
    product = weights * d_weights
    d_logits = product - weights * dot(
        dot(product, member, 1, 1, exact), member, 1, 0, exact
    )
    small[0] = d_logits
    for h in range(heads):
        part = slice(h * width, (h + 1) * width)
        normed = scores[part, :]
        sig = jax.nn.sigmoid(normed)
        gate = 0.2 + 0.8 * sig
        d_logit = small[0, h:h + 1, :]
        d_alphas[:, h:h + 1] = jnp.sum(normed * gate * d_logit, axis=1, keepdims=True)
        d_norm = d_logit * alphas[:, h:h + 1] * (gate + 0.8 * normed * sig * (1.0 - sig))
        first = jnp.mean(d_norm, axis=0, keepdims=True)
        second = jnp.mean(d_norm * normed, axis=0, keepdims=True)
        d_score = small[1, h:h + 1, :] * (d_norm - first - normed * second)
        dmixed[5 * hidden + h * width:5 * hidden + (h + 1) * width, :] = d_score.astype(BF16)
        scores[part, :] = d_score
    for j in range(pieces):
        ga_ref[j] = d_alphas[j * piece_rows:(j + 1) * piece_rows, :].astype(BF16)
    dmixed[:5 * hidden, :] = dhid[0:5].reshape(5 * hidden, edges)

    d_per_atom = dot(member, scores[...], 1, 1, exact).astype(BF16)
    gt_ref[...] = dot(ext_ref[:atoms, :channels], d_per_atom, 0, 0).astype(BF16)
    d_target = dot(d_per_atom, wt_ref[...], 1, 1)

    gz_ref[...] = dot(zero_in, dmixed[...], 1, 1).astype(BF16)
    dturned[0:5] = dot(wz_ref[...], dmixed[...], 1, 0).reshape(5, channels, edges)

    def pair(first, count, re_ref, im_ref, gre_ref, gim_ref, pos, neg):
        middle = first + count
        last = middle + count
        up = dhid[first:middle].reshape(count * hidden, edges)
        down = dhid[middle:last].reshape(count * hidden, edges)
        gre_ref[...] = (dot(pos, up, 1, 1) + dot(neg, down, 1, 1)).astype(BF16)
        gim_ref[...] = (dot(pos, down, 1, 1) - dot(neg, up, 1, 1)).astype(BF16)
        dturned[first:middle] = (
            dot(re_ref[...], up, 1, 0) + dot(im_ref[...], down, 1, 0)
        ).reshape(count, channels, edges)
        dturned[middle:last] = (
            dot(re_ref[...], down, 1, 0) - dot(im_ref[...], up, 1, 0)
        ).reshape(count, channels, edges)

    pair(5, 4, w1r_ref, w1i_ref, g1r_ref, g1i_ref, one_pos, one_neg)
    pair(13, 3, w2r_ref, w2i_ref, g2r_ref, g2i_ref, two_pos, two_neg)

    def turn_back(i, carry):
        part = pl.ds(pl.multiple_of(i * BLOCK_C, BLOCK_C), BLOCK_C)
        dxs[0, part, :] = dturned[0, part, :].astype(BF16)
        for degree in DEGREES:
            for n in range(2 * degree + 1):
                total = None
                for azimuth in orders(degree):
                    k = rot_row(degree, azimuth, n)
                    term = rotf[k:k + 1, :] * dturned[slot(degree, azimuth), part, :]
                    total = term if total is None else total + term
                dxs[degree * degree + n, part, :] = total.astype(BF16)
        return carry

    lax.fori_loop(0, channels // BLOCK_C, turn_back, 0)

    ext_grad = dot(src_hot, dxs[...].reshape(25 * channels, edges), 1, 1)
    own_ref[...] = ext_grad[:atoms]
    own_ref[:, :channels] = ext_grad[:atoms, :channels] + d_target
    slots = ghost_ref.shape[1]
    for side in range(2):
        begin = atoms + side * slots
        ghost_ref[side] = ext_grad[begin:begin + slots].astype(BF16)


def compute(features, near, cot, rotation, src, tgt, wz, w1r, w1i, w2r, w2i, wt, alpha):
    edges, entries = rotation.shape
    atoms = cot.shape[0]
    pieces, piece_rows, heads = alpha.shape
    head_width = pieces * piece_rows
    channels = wt.shape[0]
    hidden = w1r.shape[1] // 4
    shape = jax.ShapeDtypeStruct
    vmem = pl.BlockSpec(memory_space=pltpu.VMEM)
    out_shape = (
        shape((atoms, 25 * hidden), BF16),
        shape((atoms, 25 * channels), F32),
        shape(near.shape, BF16),
        shape(wz.shape, BF16),
        shape(w1r.shape, BF16),
        shape(w1i.shape, BF16),
        shape(w2r.shape, BF16),
        shape(w2i.shape, BF16),
        shape(wt.shape, BF16),
        shape(alpha.shape, BF16),
    )
    scratch = [
        pltpu.VMEM((atoms + 2 * near.shape[1], 25 * channels), BF16),
        pltpu.VMEM((head_width, heads), F32),
        pltpu.VMEM((head_width, heads), F32),
        pltpu.VMEM((entries, edges), F32),
        pltpu.VMEM((25, channels, edges), F32),
        pltpu.VMEM((19, channels, edges), BF16),
        pltpu.VMEM((19, hidden, edges), F32),
        pltpu.VMEM((25, hidden, edges), BF16),
        pltpu.VMEM((25, hidden, edges), F32),
        pltpu.VMEM((head_width * heads, edges), F32),
        pltpu.VMEM((19, hidden, edges), BF16),
        pltpu.VMEM((wz.shape[1], edges), BF16),
        pltpu.VMEM((19, channels, edges), F32),
        pltpu.VMEM((25, channels, edges), BF16),
        pltpu.VMEM((2, heads, edges), F32),
        pltpu.VMEM((2, hidden, edges), F32),
    ]
    return pl.pallas_call(
        compute_kernel,
        out_shape=out_shape,
        in_specs=[vmem] * 13,
        out_specs=[vmem] * 10,
        scratch_shapes=scratch,
        compiler_params=pltpu.CompilerParams(vmem_limit_bytes=56 * 2**20),
        name="slab",
    )(features, near, cot, rotation, src, tgt, wz, w1r, w1i, w2r, w2i, wt, alpha)


MESH = pl.DeviceIdType.MESH


def greet(n, depth):
    me = lax.axis_index("graph")
    row = lax.axis_index("dp")
    barrier = pltpu.get_barrier_semaphore()
    for d in range(1, n):
        pl.semaphore_signal(
            barrier, inc=1, device_id=(row, lax.rem(me + d, n)), device_id_type=MESH)
    for d in range(1, depth):
        pl.semaphore_signal(
            barrier, inc=1, device_id=(lax.rem(row + d, depth), me), device_id_type=MESH)
    pl.semaphore_wait(barrier, n - 1 + depth - 1)


def gather_kernel(n, count, *refs):
    shards = refs[:count]
    feat_ref, left_ref, right_ref = refs[count:count + 3]
    full = refs[count + 3:2 * count + 3]
    ghosts = refs[2 * count + 3]
    outgoing, send_sem, recv_sem, pass_sem, local_sem, side_send, side_recv = refs[2 * count + 4:]
    me = lax.axis_index("graph")
    row = lax.axis_index("dp")
    half = n // 2
    sibling = me + 1 - 2 * lax.rem(me, 2)
    right, left = lax.rem(me + 1, n), lax.rem(me + n - 1, n)
    own = feat_ref[...].astype(BF16)
    for side, list_ref in ((0, left_ref), (1, right_ref)):
        ids = lax.broadcasted_iota(jnp.int32, (own.shape[0], list_ref.shape[1]), 0)
        pick = (ids == list_ref[...]).astype(F32).astype(BF16)
        outgoing[side] = dot(pick, own, 0, 0).astype(BF16)
    greet(n, 1)

    def remote(src, dst, send, recv, target):
        copy = pltpu.make_async_remote_copy(
            src_ref=src, dst_ref=dst, send_sem=send, recv_sem=recv,
            device_id=(row, target), device_id_type=MESH)
        copy.start()
        return copy

    sends = []
    direct = []
    for d in range(1, half):
        target = lax.rem(me + 2 * d, n)
        for w in range(count):
            direct.append(remote(shards[w], full[w].at[me], send_sem.at[d, w],
                                 recv_sem.at[d, w], target))
    locals_ = []
    for w in range(count):
        copy = pltpu.make_async_copy(shards[w], full[w].at[me], local_sem.at[w])
        copy.start()
        locals_.append(copy)
        sends.append(remote(shards[w], full[w].at[me], send_sem.at[0, w],
                            recv_sem.at[0, w], sibling))
    for side, target in ((1, left), (0, right)):
        sends.append(remote(outgoing.at[1 - side], ghosts.at[side], side_send.at[side],
                            side_recv.at[side], target))
    for d in range(1, half):
        source = lax.rem(me + n - 2 * d, n)
        for w in range(count):
            direct[(d - 1) * count + w].wait_recv()
            sends.append(remote(full[w].at[source], full[w].at[source], pass_sem.at[0, d, w],
                                pass_sem.at[1, d, w], sibling))
    for copy in direct:
        copy.wait_send()
    for copy in locals_:
        copy.wait()
    for copy in sends:
        copy.wait()


def gather(n, shards, features, send_left, send_right):
    count = len(shards)
    vmem = pl.BlockSpec(memory_space=pltpu.VMEM)
    shapes = [jax.ShapeDtypeStruct((n, *s.shape), s.dtype) for s in shards]
    ghosts = (2, send_left.shape[1], features.shape[1])
    shapes.append(jax.ShapeDtypeStruct(ghosts, BF16))
    dma = pltpu.SemaphoreType.DMA
    return pl.pallas_call(
        partial(gather_kernel, n, count),
        out_shape=tuple(shapes),
        in_specs=[vmem] * (count + 3),
        out_specs=[vmem] * (count + 1),
        scratch_shapes=[pltpu.VMEM(ghosts, BF16),
                        dma((n // 2, count)), dma((n // 2, count)), dma((2, n // 2, count)),
                        dma((count,)), dma((2,)), dma((2,))],
        compiler_params=pltpu.CompilerParams(collective_id=0, has_side_effects=True),
        name="fetch",
    )(*shards, features, send_left, send_right)


def reduce_kernel(n, depth, count, *refs):
    terms = refs[:count]
    ghosts = refs[count]
    final = refs[count + 1:2 * count + 1]
    back = refs[2 * count + 1]
    rest = refs[2 * count + 2:]
    landed = rest[:count]
    partial_sums = rest[count:2 * count]
    arrived = rest[2 * count:3 * count]
    layers = rest[3 * count:4 * count]
    incoming = rest[4 * count:5 * count]
    (core_send, core_recv, chip_send, chip_recv, deep_send, deep_recv, last_send, last_recv,
     side_send, side_recv) = rest[5 * count:]
    me = lax.axis_index("graph")
    row = lax.axis_index("dp")
    half = n // 2
    parity = lax.rem(me, 2)
    chip = lax.div(me, 2)
    sibling = me + 1 - 2 * parity
    right, left = lax.rem(me + 1, n), lax.rem(me + n - 1, n)
    greet(n, depth)

    def remote(src, dst, send, recv, target):
        copy = pltpu.make_async_remote_copy(
            src_ref=src, dst_ref=dst, send_sem=send, recv_sem=recv,
            device_id=target, device_id_type=MESH)
        copy.start()
        return copy

    order = list(range(1, half)) + [0]
    first, second, third, fourth = {}, {}, {}, {}
    for w in range(count):
        for d in order:
            spot = lax.rem(chip + d, half)
            first[d, w] = remote(
                terms[w].at[2 * spot + 1 - parity], landed[w].at[d],
                core_send.at[d, w], core_recv.at[d, w], (row, sibling))
    for w in range(count):
        for d in order:
            target = lax.rem(me + 2 * d, n)
            first[d, w].wait_recv()
            partial_sums[w][d] = (
                terms[w][target].astype(F32) + landed[w][d].astype(F32)
            ).astype(BF16)
            if d:
                second[d, w] = remote(
                    partial_sums[w].at[d], arrived[w].at[d],
                    chip_send.at[d, w], chip_recv.at[d, w], (row, target))
    sides = [
        remote(ghosts.at[0], back.at[0], side_send.at[0], side_recv.at[0], (row, left)),
        remote(ghosts.at[1], back.at[1], side_send.at[1], side_recv.at[1], (row, right)),
    ]
    split = [final[w].shape[1] != terms[w].shape[1]
             for w in range(count)]
    def sum_chips(w):
        total = partial_sums[w][0].astype(F32)
        for d in range(1, half):
            second[d, w].wait_recv()
            total = total + arrived[w][d].astype(F32)
        if split[w]:
            size = total.shape[0] // depth
            for k in range(depth):
                layers[w][k] = total[k * size:(k + 1) * size].astype(BF16)
            for z in range(1, depth):
                target = lax.rem(row + z, depth)
                third[z, w] = remote(
                    layers[w].at[target], incoming[w].at[z],
                    deep_send.at[z, w], deep_recv.at[z, w], (target, me))
        else:
            final[w][row] = total.astype(BF16)

    def sum_depth(w):
        if split[w]:
            total = layers[w][row].astype(F32)
            for z in range(1, depth):
                third[z, w].wait_recv()
                total = total + incoming[w][z].astype(F32)
            final[w][row] = total.astype(BF16)
        for z in range(1, depth):
            fourth[z, w] = remote(
                final[w].at[row], final[w].at[row],
                last_send.at[z, w], last_recv.at[z, w], (lax.rem(row + z, depth), me))

    lag = min(4, count)
    for w in range(count + lag):
        if w < count:
            sum_chips(w)
        if w >= lag:
            sum_depth(w - lag)
    for group in (first, second, third):
        for copy in group.values():
            copy.wait_send()
    for copy in sides:
        copy.wait()
    for copy in fourth.values():
        copy.wait()


def reduce(n, depth, terms, ghosts):
    count = len(terms)
    half = n // 2
    vmem = pl.BlockSpec(memory_space=pltpu.VMEM)

    def layered(t):
        rows = t.shape[1] if t.shape[1] % depth else t.shape[1] // depth
        return (depth, rows, t.shape[2])

    shapes = [jax.ShapeDtypeStruct(layered(t), BF16) for t in terms]
    shapes.append(jax.ShapeDtypeStruct(ghosts.shape, ghosts.dtype))
    dma = pltpu.SemaphoreType.DMA
    scratch = [pltpu.VMEM((half, *t.shape[1:]), BF16) for _ in range(3) for t in terms]
    scratch += [pltpu.VMEM(layered(t), BF16) for _ in range(2) for t in terms]
    scratch += [dma((half, count)) for _ in range(4)]
    scratch += [dma((depth, count)) for _ in range(4)]
    scratch += [dma((2,)), dma((2,))]
    return pl.pallas_call(
        partial(reduce_kernel, n, depth, count),
        out_shape=tuple(shapes),
        in_specs=[vmem] * (count + 1),
        out_specs=[vmem] * (count + 1),
        scratch_shapes=scratch,
        compiler_params=pltpu.CompilerParams(collective_id=1, has_side_effects=True),
        name="combine",
    )(*terms, ghosts)


def finish_kernel(count, *refs):
    own_ref, back_ref, left_ref, right_ref = refs[:4]
    final = refs[4:4 + count]
    out_ref = refs[4 + count]
    grads = refs[5 + count:]
    total = own_ref[...]
    for side, list_ref in ((0, right_ref), (1, left_ref)):
        ids = lax.broadcasted_iota(jnp.int32, (total.shape[0], list_ref.shape[1]), 0)
        put = (ids == list_ref[...]).astype(F32).astype(BF16)
        total = total + dot(put, back_ref[side], 1, 0)
    out_ref[...] = total
    for source, grad in zip(final, grads):
        depth, size = source.shape[:2]
        if size == grad.shape[0]:
            value = source[0].astype(F32)
            for k in range(1, depth):
                value = value + source[k].astype(F32)
            grad[...] = value
        else:
            for k in range(depth):
                grad[k * size:(k + 1) * size, :] = source[k].astype(F32)


def finish(own, back, send_left, send_right, final, weights):
    count = len(final)
    vmem = pl.BlockSpec(memory_space=pltpu.VMEM)
    shapes = [jax.ShapeDtypeStruct(own.shape, F32)]
    shapes += [jax.ShapeDtypeStruct(w.shape, F32) for w in weights]
    return pl.pallas_call(
        partial(finish_kernel, count),
        out_shape=tuple(shapes),
        in_specs=[vmem] * (count + 4),
        out_specs=[vmem] * (count + 1),
        name="finish",
    )(own, back, send_left, send_right, *final)


def body(n, depth, features, cotangent, rotation, send_left, send_right, edge_src, edge_tgt,
         *weights):
    *full, near = gather(n, weights, features[0], send_left, send_right)
    matrices = [f.reshape(-1, f.shape[2]) for f in full[:6]]
    attended, own_grad, ghost_grad, *terms = compute(
        features[0], near, cotangent[0], rotation[0].T, edge_src, edge_tgt, *matrices, full[6])
    terms = [t.reshape(n, -1, t.shape[-1]) for t in terms]
    *final, back = reduce(n, depth, terms, ghost_grad)
    grad_features, *grads = finish(own_grad, back, send_left, send_right, final, weights)
    return (attended[None], grad_features[None], *grads)


def solution(mesh):
    cell = P("dp", "graph", None)
    lists = P("dp", "graph")
    shard = P("graph", None)
    in_specs = (cell, cell, P("dp", None, "graph")) + (lists,) * 4 + (shard,) * 7
    out_specs = (cell, cell) + (shard,) * 7
    return jax.shard_map(
        partial(body, mesh.shape["graph"], mesh.shape["dp"]), mesh=mesh,
        in_specs=in_specs, out_specs=out_specs, check_vma=False)
```
